1024 devices in a mesh: plane: 128 (over z, x, y_hi), span: 8 (over y_lo, core).
Axes of the slice: x: 4, y: 8 (y_hi: 2, y_lo: 4; y = y_hi * 4 + y_lo), z: 16, core: 2. Of those that a mesh axis runs over, the one named last changes fastest.
Arguments:
- pressure_source: float32 [512, 512, 1024], P('span', 'plane'), may hold values from -24 to 24
- solid_mask: int32 [512, 1024], P('plane'), may hold values from 0 to 1, as said below
Outputs:
- pressure: float32 [512, 512, 1024], P('span', 'plane')
The draws below stay inside these ranges and needn't reach their ends.
Inputs may be any that keep to these rules, and one draw needn't show every extreme that they name: `solid_mask`: 1 where a plane cell lies inside a tube of a staggered bank of tubes, else 0.
All inputs are finite; a program needn't handle non-finite values.
Results may differ from the reference program's by a relative error of at most 0.0001.
Values sent between devices are 32-bit elements; how exact they have to be, the bound alone decides.
A program may use at most 32 MiB of HBM per device.

```python
import jax
import jax.numpy as jnp
from jax import lax

NS = 512
NY = 1024
NX = 512


def draw_solid_mask(key, part):
    pitch = max(NY // 40, 4)
    key_offset, key_radius = jax.random.split(jax.random.fold_in(key, 7))
    offset = jax.random.randint(key_offset, (), 0, pitch)
    row_tubes = NX // pitch + 3
    column_tubes = NY // pitch + 2
    radii = jax.random.randint(key_radius, (row_tubes, column_tubes), pitch // 4, pitch // 2 + 1)
    row_pos = jnp.broadcast_to(jnp.arange(NX, dtype=jnp.int32)[:, None], (NX, NY))
    column_pos = jnp.broadcast_to(jnp.arange(NY, dtype=jnp.int32)[None, :], (NX, NY))
    column_tube = column_pos // pitch
    row_shift = column_tube % 2 * (pitch // 2) + offset
    row_tube = (row_pos - row_shift) // pitch
    center_row = row_tube * pitch + row_shift + pitch // 2
    center_column = column_tube * pitch + pitch // 2
    tube_radius = radii[jnp.clip(row_tube + 1, 0, row_tubes - 1), column_tube]
    row_gap = row_pos - center_row
    column_gap = column_pos - center_column
    inside = row_gap * row_gap + column_gap * column_gap <= tube_radius * tube_radius
    return inside.astype(jnp.int32)


def block_levels(own_key, extent, cuts, smallest, high):
    level = 1.0
    for axis_at, parts in cuts:
        steps = jax.random.uniform(jax.random.fold_in(jax.random.fold_in(own_key, 6), axis_at), (parts,), jnp.float32, smallest / len(cuts), high / len(cuts))
        level = level * jnp.repeat(jnp.exp(steps), extent[axis_at] // parts).reshape((-1,) + (1,) * (len(extent) - 1 - axis_at))
    return level


def bell_draw(key, extent, spread, reach, cuts=(), kind=jnp.bfloat16):
    result = jax.random.normal(key, extent, jnp.float32) * spread
    if len(cuts) > 0:
        result = block_levels(key, extent, cuts, -0.22, 0.18) * result
    return jnp.clip(result, min=-reach, max=reach).astype(kind)


def setup_inputs(seed: int = 0) -> dict:
    key_of = jax.random.split(jax.random.key(seed), 3)
    return {
        "pressure_source": bell_draw(key_of[0], (NS, NX, NY), 4.0, 24.0, ((0, 8), (1, 128)), jnp.float32),
        "solid_mask": draw_solid_mask(jax.random.fold_in(key_of[2], 71), 0),
    }


PENALTY = 12.0


def tables(length):
    nyquist = length // 2
    modes = jnp.arange(length, dtype=jnp.int32)
    wavenumber = jnp.where(modes <= nyquist, modes, modes - nyquist).astype(jnp.int32)
    points = jnp.arange(length, dtype=jnp.int32)
    phases = (points[:, None] * wavenumber[None, :]) % length
    angles = phases.astype(jnp.float32) * jnp.float32(2.0 * jnp.pi / length)
    cosine_mode = modes <= nyquist
    forward = jnp.where(cosine_mode[None, :], jnp.cos(angles), jnp.sin(angles))
    weight = jnp.where(cosine_mode & ((wavenumber == 0) | (wavenumber == nyquist)), jnp.float32(1.0), jnp.float32(2.0)) / jnp.float32(length)
    inverse = (forward * weight[None, :]).T
    eigen_values = 2.0 - 2.0 * jnp.cos(wavenumber.astype(jnp.float32) * jnp.float32(2.0 * jnp.pi / length))
    kept = jnp.where(3 * wavenumber <= length, jnp.float32(1.0), jnp.float32(0.0))
    return forward * kept[None, :], inverse, eigen_values


def reference(pressure_source, solid_mask):
    forward, inverse, eigen_values = tables(NS)
    penalty = solid_mask.astype(jnp.float32) * PENALTY
    block_size = min(64, NS)
    block_count = NS // block_size
    forward_blocks = forward.reshape(NS, block_count, block_size).transpose(1, 0, 2)
    inverse_blocks = inverse.reshape(block_count, block_size, NS)
    eigen_blocks = eigen_values.reshape(block_count, block_size)

    def sweep_block(running, block_tables):
        forward_part, inverse_part, eigen_part = block_tables
        spectrum = jnp.einsum("sm,sxy->mxy", forward_part, pressure_source, precision=lax.Precision.HIGHEST)
        diagonal = 4.0 + eigen_part[:, None, None] + penalty[None]
        sweep_one = spectrum / diagonal
        padded = jnp.pad(sweep_one, ((0, 0), (1, 1), (1, 1)))
        beside_all = padded[:, :-2, 1:-1] + padded[:, 2:, 1:-1] + padded[:, 1:-1, :-2] + padded[:, 1:-1, 2:]
        sweep_two = (spectrum + beside_all) / diagonal
        running = running + jnp.einsum("ms,mxy->sxy", inverse_part, sweep_two, precision=lax.Precision.HIGHEST)
        return running, None

    start_field = jnp.zeros(pressure_source.shape, jnp.float32)
    pressure, _ = lax.scan(sweep_block, start_field, (forward_blocks, inverse_blocks, eigen_blocks))
    return pressure
```

```python
import functools

import jax
import jax.numpy as jnp
import ml_dtypes
import numpy as np
from jax import lax
from jax.experimental import pallas as pl
from jax.experimental.pallas import tpu as pltpu
from jax.sharding import PartitionSpec as P

MESH = pl.DeviceIdType.MESH
NS = 512
MODES = 352
PENALTY = 12.0
ROWS = (0, 3, 1, 2)
F32, BF16 = jnp.float32, jnp.bfloat16


def tables():
    modes = np.arange(NS)
    wave = np.where(modes <= NS // 2, modes, modes - NS // 2)
    kept = np.nonzero(3 * wave <= NS)[0]
    wave, cosine = wave[kept], kept <= NS // 2
    angle = (np.arange(NS)[None, :] * wave[:, None] % NS) * (2.0 * np.pi / NS)
    forward = np.zeros((MODES, NS))
    forward[: len(kept)] = np.where(cosine[:, None], np.cos(angle), np.sin(angle))
    weight = np.where(cosine & ((wave == 0) | (wave == NS // 2)), 1.0, 2.0) / NS
    inverse = np.zeros((NS, MODES))
    inverse[:, : len(kept)] = (forward[: len(kept)] * weight[:, None]).T
    eigen = np.zeros(MODES)
    eigen[: len(kept)] = 2.0 - 2.0 * np.cos(wave * (2.0 * np.pi / NS))
    scale = np.stack([1.0 / (4.0 + eigen), 1.0 / (4.0 + eigen + PENALTY)])
    scale = np.broadcast_to(scale[:, :, None], (2, MODES, 128))

    def halves(x):
        high = x.astype(ml_dtypes.bfloat16)
        return np.stack([high, (x - high.astype(np.float64)).astype(ml_dtypes.bfloat16)])

    return halves(forward), halves(inverse), np.ascontiguousarray(scale, dtype=np.float32)


def split(x):
    high = x.astype(BF16)
    return high, (x - high.astype(F32)).astype(BF16)


def dot(a, b):
    return jnp.dot(a, b, preferred_element_type=F32)


def kernel(planes, x_ref, mask_ref, f_hbm, g_hbm, d_hbm, out_ref, xr, xh, xl, fv, gv, dv, sv, s1,
           hrow, ecol, hcol, s2h, s2l, yv, mv, gsend, grecv, rsend, rrecv, hsend, hrecv, msem, lsem):
    p, q = lax.axis_index("plane"), lax.axis_index("span")
    pair, half = p // 2, p % 2
    mine = q % 2
    col = half * 4 + q // 2
    row = pair * 2 + mine
    keeps = half == mine

    def worker(block_row, block_col):
        return block_row // 2 * 2 + block_col // 4, block_col % 4 * 2 + block_row % 2

    tables_in = [
        pltpu.make_async_copy(src, dst, lsem.at[i])
        for i, (src, dst) in enumerate(((f_hbm, fv), (g_hbm, gv), (d_hbm, dv)))
    ]
    for copy in tables_in:
        copy.start()

    barrier = pltpu.get_barrier_semaphore()
    for i in range(1, 16):
        at = (half * 8 + q + i) % 16
        pl.semaphore_signal(barrier, inc=1, device_id=(pair * 2 + at // 8, at % 8), device_id_type=MESH)
    outer = row + 2 * mine - 1
    has_outer = (outer >= 0) & (outer < planes)

    @pl.when(has_outer)
    def _():
        pl.semaphore_signal(barrier, inc=1, device_id=worker(outer, col), device_id_type=MESH)

    pl.semaphore_wait(barrier, jnp.where(has_outer, 16, 15))

    def lanes(c):
        return pl.ds(pl.multiple_of(c * 128, 128), 128)

    def gather(c, source):
        plane, span = worker(pair * 2 + half, c)
        return pltpu.make_async_remote_copy(
            src_ref=x_ref.at[:, :, lanes(c)], dst_ref=xr.at[source], send_sem=gsend.at[c],
            recv_sem=grecv.at[source], device_id=(plane, span), device_id_type=MESH)

    def gather_own():
        return pltpu.make_async_copy(x_ref.at[:, :, lanes(col)], xr.at[q], lsem.at[3])

    for d in (4, 3, 5, 2, 6, 1, 7):
        gather((col + d) % 8, q).start()

    mask_own = pltpu.make_async_copy(mask_ref.at[:, lanes(col)], mv, lsem.at[4])
    mask_sent = pltpu.make_async_remote_copy(
        src_ref=mask_ref.at[:, lanes((col + 4) % 8)], dst_ref=mv, send_sem=msem.at[0], recv_sem=msem.at[1],
        device_id=(pair * 2 + 1 - half, q), device_id_type=MESH)

    @pl.when(keeps)
    def _():
        gather_own().start()
        mask_own.start()
        mask_sent.start()

    @pl.when(jnp.logical_not(keeps))
    def _():
        gather(col, q).start()

    for copy in tables_in:
        copy.wait()

    @pl.when(keeps)
    def _():
        mask_own.wait()

    @pl.when(jnp.logical_not(keeps))
    def _():
        mask_sent.wait_recv()

    for i in range(8):
        own = keeps & (q == i)

        @pl.when(own)
        def _():
            gather_own().wait()

        @pl.when(jnp.logical_not(own))
        def _():
            gather(0, i).wait_recv()

        for at, r in enumerate(ROWS):
            high, low = split(xr[i, :, r, :])
            xh[i * 64 : i * 64 + 64, at * 128 : at * 128 + 128] = high
            xl[i * 64 : i * 64 + 64, at * 128 : at * 128 + 128] = low

    def halo(i):
        step = 2 * (i % 2) - 1
        to_row, to_col = (row + step, col) if i < 2 else (row, col + step)
        exists = (to_row >= 0) & (to_row < planes) & (to_col >= 0) & (to_col < 8)
        src = s1.at[3 * i] if i < 2 else ecol.at[i - 2]
        dst = hrow.at[1 - i] if i < 2 else hcol.at[3 - i]
        back = i // 2 * 2 + 1 - i % 2
        return exists, lambda: pltpu.make_async_remote_copy(
            src_ref=src, dst_ref=dst, send_sem=hsend.at[i], recv_sem=hrecv.at[back],
            device_id=worker(to_row, to_col), device_id_type=MESH)

    def send_halo(i):
        exists, copy = halo(i)

        @pl.when(exists)
        def _():
            copy().start()

    for h in range(2):
        at = slice(h * 256, h * 256 + 256)
        spectrum = dot(fv[0], xh[:, at]) + dot(fv[1], xh[:, at]) + dot(fv[0], xl[:, at])
        for j in range(2):
            r = ROWS[2 * h + j]
            part = spectrum[:, j * 128 : j * 128 + 128]
            sv[:, r * 128 : r * 128 + 128] = part
            s1[r] = part * jnp.where(mv[r : r + 1, :] != 0, dv[1], dv[0])
        if h == 0:
            send_halo(0)
            send_halo(1)

    lane = lax.broadcasted_iota(jnp.int32, (16, 128), 1)
    line = lax.broadcasted_iota(jnp.int32, (16, 128), 0)
    edge = jnp.where(line < 8, 0, 127)

    def pick(r):
        return jnp.where((line % 8 == r) & (lane == edge), 1.0, 0.0).astype(BF16)

    edges = jnp.zeros((16, MODES), F32)
    for r in range(4):
        for part in split(s1[r]):
            edges += lax.dot_general(pick(r), part, (((1,), (1,)), ((), ())), preferred_element_type=F32)
    ecol[0] = edges[:8]
    ecol[1] = edges[8:]
    send_halo(2)
    send_halo(3)

    wide = lax.broadcasted_iota(jnp.int32, (MODES, 128), 1)
    for r in range(4):
        here = s1[r]
        total = sv[:, r * 128 : r * 128 + 128]
        total += jnp.where(wide == 0, 0.0, pltpu.roll(here, 1, 1))
        total += jnp.where(wide == 127, 0.0, pltpu.roll(here, 127, 1))
        if r > 0:
            total += s1[r - 1]
        if r < 3:
            total += s1[r + 1]
        sv[:, r * 128 : r * 128 + 128] = total

    for i in range(4):
        exists, copy = halo(i)
        dst = hrow.at[i] if i < 2 else hcol.at[i - 2]

        @pl.when(exists)
        def _():
            pltpu.make_async_remote_copy(
                src_ref=dst, dst_ref=dst, send_sem=hsend.at[i], recv_sem=hrecv.at[i],
                device_id=(p, q), device_id_type=MESH).wait_recv()

        @pl.when(jnp.logical_not(exists))
        def _():
            dst[...] = jnp.zeros(dst.shape, F32)

    columns = split(jnp.concatenate([hcol[0], hcol[1]], axis=0).T)
    for r in range(4):
        total = sv[:, r * 128 : r * 128 + 128]
        if r == 0:
            total += hrow[0]
        if r == 3:
            total += hrow[1]
        place = pick(r)
        for part in columns:
            total += dot(part, place)
        total *= jnp.where(mv[r : r + 1, :] != 0, dv[1], dv[0])
        high, low = split(total)
        s2h[:, r * 128 : r * 128 + 128] = high
        s2l[:, r * 128 : r * 128 + 128] = low

    def scatter(target, c):
        return pltpu.make_async_remote_copy(
            src_ref=yv.at[target], dst_ref=out_ref.at[:, :, lanes(c)], send_sem=rsend.at[target],
            recv_sem=rrecv.at[c], device_id=(pair * 2 + mine, target), device_id_type=MESH)

    def scatter_own():
        return pltpu.make_async_copy(yv.at[q], out_ref.at[:, :, lanes(col)], lsem.at[5])

    first = q // 2 + jnp.where(keeps, 2, 0)
    for k in range(4):
        j = (first + k) % 4
        cells = pl.ds(pl.multiple_of(j * 128, 128), 128)
        field = dot(gv[0, cells, :], s2h[...]) + dot(gv[1, cells, :], s2h[...]) + dot(gv[0, cells, :], s2l[...])
        for core in range(2):
            target = j * 2 + core
            own = keeps & (target == q)
            for r in range(4):
                yv[target, :, r, :] = field[core * 64 : core * 64 + 64, r * 128 : r * 128 + 128]

            @pl.when(own)
            def _():
                scatter_own().start()

            @pl.when(jnp.logical_not(own))
            def _():
                scatter(target, col).start()

    for c in range(8):
        own = keeps & (c == col)

        @pl.when(own)
        def _():
            scatter_own().wait()

        @pl.when(jnp.logical_not(own))
        def _():
            scatter(0, c).wait_recv()
            gather(c, q).wait_send()

    for target in range(8):
        @pl.when(jnp.logical_not(keeps & (target == q)))
        def _():
            scatter(target, col).wait_send()

    for i in range(4):
        exists, copy = halo(i)

        @pl.when(exists)
        def _():
            copy().wait_send()

    @pl.when(keeps)
    def _():
        mask_sent.wait_send()


def local(planes, consts, pressure_source, solid_mask):
    anywhere = pl.BlockSpec(memory_space=pl.ANY)
    dma = pltpu.SemaphoreType.DMA
    return pl.pallas_call(
        functools.partial(kernel, planes),
        out_shape=jax.ShapeDtypeStruct(pressure_source.shape, F32),
        in_specs=[anywhere] * 5,
        out_specs=anywhere,
        scratch_shapes=[
            pltpu.VMEM((8, 64, 4, 128), F32),
            pltpu.VMEM((NS, 512), BF16),
            pltpu.VMEM((NS, 512), BF16),
            pltpu.VMEM((2, MODES, NS), BF16),
            pltpu.VMEM((2, NS, MODES), BF16),
            pltpu.VMEM((2, MODES, 128), F32),
            pltpu.VMEM((MODES, 512), F32),
            pltpu.VMEM((4, MODES, 128), F32),
            pltpu.VMEM((2, MODES, 128), F32),
            pltpu.VMEM((2, 8, MODES), F32),
            pltpu.VMEM((2, 8, MODES), F32),
            pltpu.VMEM((MODES, 512), BF16),
            pltpu.VMEM((MODES, 512), BF16),
            pltpu.VMEM((8, 64, 4, 128), F32),
            pltpu.VMEM((4, 128), jnp.int32),
            dma((8,)), dma((8,)), dma((8,)), dma((8,)), dma((4,)), dma((4,)), dma((2,)), dma((6,)),
        ],
        compiler_params=pltpu.CompilerParams(
            collective_id=0, has_side_effects=True, vmem_limit_bytes=60 * 1024 * 1024),
    )(pressure_source, solid_mask, *consts)


def solution(mesh):
    consts = tables()

    def step(pressure_source, solid_mask):
        return local(mesh.shape["plane"], [jnp.asarray(c) for c in consts], pressure_source, solid_mask)

    return jax.shard_map(
        step, mesh=mesh, in_specs=(P("span", "plane", None), P("plane", None)),
        out_specs=P("span", "plane", None), check_vma=False)
```

```python
import functools

import jax
import jax.numpy as jnp
import ml_dtypes
import numpy as np
from jax import lax
from jax.experimental import pallas as pl
from jax.experimental.pallas import tpu as pltpu
from jax.sharding import PartitionSpec as P

MESH = pl.DeviceIdType.MESH
NS = 512
MODES = 352
PENALTY = 12.0
IN = ((0, 2), (2, 1), (3, 1))
OUT = ((0, 1), (1, 1), (2, 2))
F32, BF16 = jnp.float32, jnp.bfloat16


def tables():
    modes = np.arange(NS)
    wave = np.where(modes <= NS // 2, modes, modes - NS // 2)
    kept = np.nonzero(3 * wave <= NS)[0]
    wave, cosine = wave[kept], kept <= NS // 2
    angle = (np.arange(NS)[None, :] * wave[:, None] % NS) * (2.0 * np.pi / NS)
    forward = np.zeros((MODES, NS))
    forward[: len(kept)] = np.where(cosine[:, None], np.cos(angle), np.sin(angle))
    weight = np.where(cosine & ((wave == 0) | (wave == NS // 2)), 1.0, 2.0) / NS
    inverse = np.zeros((NS, MODES))
    inverse[:, : len(kept)] = (forward[: len(kept)] * weight[:, None]).T
    eigen = np.zeros(MODES)
    eigen[: len(kept)] = 2.0 - 2.0 * np.cos(wave * (2.0 * np.pi / NS))
    scale = np.stack([1.0 / (4.0 + eigen), 1.0 / (4.0 + eigen + PENALTY)])
    scale = np.broadcast_to(scale[:, :, None], (2, MODES, 128))

    def halves(x):
        high = x.astype(ml_dtypes.bfloat16)
        return np.stack([high, (x - high.astype(np.float64)).astype(ml_dtypes.bfloat16)])

    return halves(forward), halves(inverse), np.ascontiguousarray(scale, dtype=np.float32)


def split(x):
    high = x.astype(BF16)
    return high, (x - high.astype(F32)).astype(BF16)


def dot(a, b):
    return jnp.dot(a, b, preferred_element_type=F32)


def kernel(planes, x_ref, mask_ref, f_hbm, g_hbm, d_hbm, out_ref, xr, xh, xl, fv, gv, dv, scale, sv, s1,
           hrow, ecol, hcol, s2h, s2l, yv, mv, gsend, grecv, rsend, rrecv, hsend, hrecv, msem, lsem):
    p, q = lax.axis_index("plane"), lax.axis_index("span")
    pair, half = p // 2, p % 2
    mine = q % 2
    col = half * 4 + q // 2
    row = pair * 2 + mine
    keeps = half == mine

    def worker(block_row, block_col):
        return block_row // 2 * 2 + block_col // 4, block_col % 4 * 2 + block_row % 2

    def inner(block, i):
        return jnp.where(block == 1, i, 3 - i)

    def rows(block, first, count):
        return pl.ds(jnp.where(block == 1, first, 4 - first - count), count)

    tables_in = [
        pltpu.make_async_copy(src, dst, lsem.at[i])
        for i, (src, dst) in enumerate(((f_hbm, fv), (g_hbm, gv), (d_hbm, dv)))
    ]
    for copy in tables_in:
        copy.start()

    barrier = pltpu.get_barrier_semaphore()
    for i in range(1, 16):
        at = (half * 8 + q + i) % 16
        pl.semaphore_signal(barrier, inc=1, device_id=(pair * 2 + at // 8, at % 8), device_id_type=MESH)
    outer = row + 2 * mine - 1
    has_outer = (outer >= 0) & (outer < planes)

    @pl.when(has_outer)
    def _():
        pl.semaphore_signal(barrier, inc=1, device_id=worker(outer, col), device_id_type=MESH)

    pl.semaphore_wait(barrier, jnp.where(has_outer, 16, 15))

    def gather(n, c, source, block):
        plane, span = worker(pair * 2 + half, c)
        part = rows(block, *IN[n])
        return pltpu.make_async_remote_copy(
            src_ref=x_ref.at[:, c, part], dst_ref=xr.at[source, :, part], send_sem=gsend.at[n, c],
            recv_sem=grecv.at[n, source], device_id=(plane, span), device_id_type=MESH)

    def gather_own(n):
        part = rows(half, *IN[n])
        return pltpu.make_async_copy(x_ref.at[:, col, part], xr.at[q, :, part], lsem.at[4 + n])

    def mask_own():
        return pltpu.make_async_copy(mask_ref.at[col], mv, lsem.at[3])

    def mask_sent():
        return pltpu.make_async_remote_copy(
            src_ref=mask_ref.at[(col + 4) % 8], dst_ref=mv, send_sem=msem.at[0], recv_sem=msem.at[1],
            device_id=(pair * 2 + 1 - half, q), device_id_type=MESH)

    @pl.when(keeps)
    def _():
        mask_own().start()
        mask_sent().start()

    def send_in(n):
        for d in (4, 3, 5, 2, 6, 1, 7):
            gather(n, (col + d) % 8, q, half).start()

        @pl.when(keeps)
        def _():
            gather_own(n).start()

        @pl.when(jnp.logical_not(keeps))
        def _():
            gather(n, col, q, half).start()

    send_in(0)
    send_in(1)

    for copy in tables_in:
        copy.wait()

    @pl.when(keeps)
    def _():
        mask_own().wait()

    @pl.when(jnp.logical_not(keeps))
    def _():
        mask_sent().wait_recv()

    for i in range(4):
        scale[i] = jnp.where(mv[inner(mine, i)] != 0, dv[1], dv[0])

    def receive(n):
        for i in range(8):
            own = keeps & (q == i)

            @pl.when(own)
            def _():
                gather_own(n).wait()

            @pl.when(jnp.logical_not(own))
            def _():
                gather(n, 0, i, mine).wait_recv()

            for at in range(IN[n][0], sum(IN[n])):
                high, low = split(xr[i, :, inner(mine, at), 0, :])
                xh[i * 64 : i * 64 + 64, at * 128 : at * 128 + 128] = high
                xl[i * 64 : i * 64 + 64, at * 128 : at * 128 + 128] = low

    def halo(i):
        if i < 2:
            to_row, to_col = row + (1 - 2 * mine if i == 0 else 2 * mine - 1), col
            src, dst = s1.at[3 * i], hrow.at[i]
            back = i
        else:
            to_row, to_col = row, col + 2 * (i % 2) - 1
            src, dst = ecol.at[i - 2], hcol.at[(i ^ 1) - 2]
            back = i ^ 1
        exists = (to_row >= 0) & (to_row < planes) & (to_col >= 0) & (to_col < 8)
        return exists, lambda: pltpu.make_async_remote_copy(
            src_ref=src, dst_ref=dst, send_sem=hsend.at[i], recv_sem=hrecv.at[back],
            device_id=worker(to_row, to_col), device_id_type=MESH)

    def send_halo(i):
        exists, copy = halo(i)

        @pl.when(exists)
        def _():
            copy().start()

    def take_halo(i):
        exists, _ = halo(i)
        dst = hrow.at[i] if i < 2 else hcol.at[i - 2]

        @pl.when(exists)
        def _():
            pltpu.make_async_remote_copy(
                src_ref=dst, dst_ref=dst, send_sem=hsend.at[i], recv_sem=hrecv.at[i],
                device_id=(p, q), device_id_type=MESH).wait_recv()

        @pl.when(jnp.logical_not(exists))
        def _():
            dst[...] = jnp.zeros(dst.shape, F32)

    lane = lax.broadcasted_iota(jnp.int32, (16, 128), 1)
    line = lax.broadcasted_iota(jnp.int32, (16, 128), 0)
    edge = jnp.where(line < 8, 0, 127)

    def pick(i):
        return jnp.where((line % 8 == i) & (lane == edge), 1.0, 0.0).astype(BF16)

    def lanes(i, count=1):
        return slice(i * 128, (i + count) * 128)

    def first_sweep(n):
        at = lanes(*IN[n])
        spectrum = dot(fv[0], xh[:, at]) + dot(fv[1], xh[:, at]) + dot(fv[0], xl[:, at])
        edges = jnp.zeros((16, MODES), F32)
        for j in range(IN[n][1]):
            i = IN[n][0] + j
            part = spectrum[:, lanes(j)]
            sv[:, lanes(i)] = part
            part = part * scale[i]
            s1[i] = part
            if i % 3 == 0:
                send_halo(i // 3)
            for piece in split(part):
                edges += lax.dot_general(pick(i), piece, (((1,), (1,)), ((), ())), preferred_element_type=F32)
        ecol[2 * n] = edges[:8]
        ecol[2 * n + 1] = edges[8:]
        send_halo(2 + 2 * n)
        send_halo(3 + 2 * n)

    wide = lax.broadcasted_iota(jnp.int32, (MODES, 128), 1)

    def columns(n):
        take_halo(2 + 2 * n)
        take_halo(3 + 2 * n)
        return split(jnp.concatenate([hcol[2 * n], hcol[2 * n + 1]], axis=0).T)

    def own_terms(i):
        here = s1[i]
        total = sv[:, lanes(i)]
        total += jnp.where(wide == 0, 0.0, pltpu.roll(here, 1, 1))
        total += jnp.where(wide == 127, 0.0, pltpu.roll(here, 127, 1))
        if i > 0:
            total += s1[i - 1]
        if i < 3:
            total += s1[i + 1]
        sv[:, lanes(i)] = total

    def second_sweep(i, sides):
        total = sv[:, lanes(i)]
        if i % 3 == 0:
            total += hrow[i // 3]
        for piece in sides:
            total += dot(piece, pick(i))
        high, low = split(total * scale[i])
        s2h[:, lanes(i)] = high
        s2l[:, lanes(i)] = low

    def scatter(n, target, c, block):
        part = rows(block, *OUT[n])
        return pltpu.make_async_remote_copy(
            src_ref=yv.at[target, :, part], dst_ref=out_ref.at[:, c, part], send_sem=rsend.at[n, target],
            recv_sem=rrecv.at[n, c], device_id=(pair * 2 + mine, target), device_id_type=MESH)

    def scatter_own(n):
        part = rows(mine, *OUT[n])
        return pltpu.make_async_copy(yv.at[q, :, part], out_ref.at[:, col, part], lsem.at[7 + n])

    first = q // 2 + jnp.where(keeps, 2, 0)

    def start_scatter(n, target):
        own = keeps & (target == q)

        @pl.when(own)
        def _():
            scatter_own(n).start()

        @pl.when(jnp.logical_not(own))
        def _():
            scatter(n, target, col, mine).start()

    def inverse(h, n):
        at = lanes(2 * h, 2)
        for k in range(4):
            j = (first + k) % 4
            cells = pl.ds(pl.multiple_of(j * 128, 128), 128)
            field = dot(gv[0, cells, :], s2h[:, at]) + dot(gv[1, cells, :], s2h[:, at]) + dot(gv[0, cells, :], s2l[:, at])
            for core in range(2):
                target = j * 2 + core
                for i in range(2):
                    yv[target, :, inner(mine, 2 * h + i), 0, :] = field[core * 64 : core * 64 + 64, lanes(i)]
                start_scatter(n, target)

    receive(0)
    first_sweep(0)
    send_in(2)
    own_terms(0)
    receive(1)
    first_sweep(1)
    own_terms(1)
    sides = columns(0)
    take_halo(0)
    second_sweep(0, sides)
    second_sweep(1, sides)
    inverse(0, 0)
    receive(2)
    first_sweep(2)
    for k in range(4):
        for core in range(2):
            start_scatter(1, (first + k) % 4 * 2 + core)
    own_terms(2)
    own_terms(3)
    second_sweep(2, columns(1))
    sides = columns(2)
    take_halo(1)
    second_sweep(3, sides)
    inverse(1, 2)

    for n in range(3):
        for c in range(8):
            own = keeps & (c == col)

            @pl.when(own)
            def _():
                scatter_own(n).wait()

            @pl.when(jnp.logical_not(own))
            def _():
                scatter(n, 0, c, half).wait_recv()

        for target in range(8):
            @pl.when(jnp.logical_not(keeps & (target == q)))
            def _():
                scatter(n, target, col, mine).wait_send()

    for c in range(8):
        @pl.when(jnp.logical_not(keeps & (c == col)))
        def _():
            for n in range(3):
                gather(n, c, q, half).wait_send()

    for i in range(8):
        exists, copy = halo(i)

        @pl.when(exists)
        def _():
            copy().wait_send()

    @pl.when(keeps)
    def _():
        mask_sent().wait_send()


def local(planes, consts, pressure_source, solid_mask):
    anywhere = pl.BlockSpec(memory_space=pl.ANY)
    dma = pltpu.SemaphoreType.DMA
    source = pressure_source.reshape(64, 4, 8, 128).transpose(0, 2, 1, 3).reshape(64, 8, 4, 1, 128)
    mask = solid_mask.reshape(4, 8, 128).transpose(1, 0, 2).reshape(8, 4, 1, 128)
    out = pl.pallas_call(
        functools.partial(kernel, planes),
        out_shape=jax.ShapeDtypeStruct(source.shape, F32),
        in_specs=[anywhere] * 5,
        out_specs=anywhere,
        scratch_shapes=[
            pltpu.VMEM((8, 64, 4, 1, 128), F32),
            pltpu.VMEM((NS, 512), BF16),
            pltpu.VMEM((NS, 512), BF16),
            pltpu.VMEM((2, MODES, NS), BF16),
            pltpu.VMEM((2, NS, MODES), BF16),
            pltpu.VMEM((2, MODES, 128), F32),
            pltpu.VMEM((4, MODES, 128), F32),
            pltpu.VMEM((MODES, 512), F32),
            pltpu.VMEM((4, MODES, 128), F32),
            pltpu.VMEM((2, MODES, 128), F32),
            pltpu.VMEM((6, 8, MODES), F32),
            pltpu.VMEM((6, 8, MODES), F32),
            pltpu.VMEM((MODES, 512), BF16),
            pltpu.VMEM((MODES, 512), BF16),
            pltpu.VMEM((8, 64, 4, 1, 128), F32),
            pltpu.VMEM((4, 1, 128), jnp.int32),
            dma((3, 8)), dma((3, 8)), dma((3, 8)), dma((3, 8)), dma((8,)), dma((8,)), dma((2,)), dma((10,)),
        ],
        compiler_params=pltpu.CompilerParams(
            collective_id=0, has_side_effects=True, vmem_limit_bytes=60 * 1024 * 1024),
    )(source, mask, *consts)
    return out.reshape(64, 8, 4, 128).transpose(0, 2, 1, 3).reshape(64, 4, 1024)


def solution(mesh):
    consts = tables()

    def step(pressure_source, solid_mask):
        return local(mesh.shape["plane"], [jnp.asarray(c) for c in consts], pressure_source, solid_mask)

    return jax.shard_map(
        step, mesh=mesh, in_specs=(P("span", "plane", None), P("plane", None)),
        out_specs=P("span", "plane", None), check_vma=False)
```

```python
import functools

import jax
import jax.numpy as jnp
import ml_dtypes
import numpy as np
from jax import lax
from jax.experimental import pallas as pl
from jax.experimental.pallas import tpu as pltpu
from jax.sharding import PartitionSpec as P

MESH = pl.DeviceIdType.MESH
NS = 512
MODES = 352
PENALTY = 12.0
IN = ((0, 2), (2, 1), (3, 1))
OUT = ((0, 1), (1, 1), (2, 2))
F32, BF16 = jnp.float32, jnp.bfloat16


def tables():
    modes = np.arange(NS)
    wave = np.where(modes <= NS // 2, modes, modes - NS // 2)
    kept = np.nonzero(3 * wave <= NS)[0]
    wave, cosine = wave[kept], kept <= NS // 2
    angle = (np.arange(NS)[None, :] * wave[:, None] % NS) * (2.0 * np.pi / NS)
    forward = np.zeros((MODES, NS))
    forward[: len(kept)] = np.where(cosine[:, None], np.cos(angle), np.sin(angle))
    weight = np.where(cosine & ((wave == 0) | (wave == NS // 2)), 1.0, 2.0) / NS
    inverse = np.zeros((NS, MODES))
    inverse[:, : len(kept)] = (forward[: len(kept)] * weight[:, None]).T
    eigen = np.zeros(MODES)
    eigen[: len(kept)] = 2.0 - 2.0 * np.cos(wave * (2.0 * np.pi / NS))
    scale = np.stack([1.0 / (4.0 + eigen), 1.0 / (4.0 + eigen + PENALTY)])
    scale = np.broadcast_to(scale[:, :, None], (2, MODES, 128))

    def halves(x):
        high = x.astype(ml_dtypes.bfloat16)
        return np.stack([high, (x - high.astype(np.float64)).astype(ml_dtypes.bfloat16)])

    return halves(forward), halves(inverse), np.ascontiguousarray(scale, dtype=np.float32)


def split(x):
    high = x.astype(BF16)
    return high, (x - high.astype(F32)).astype(BF16)


def dot(a, b):
    return jnp.dot(a, b, preferred_element_type=F32)


def kernel(planes, x_ref, mask_ref, f_hbm, g_hbm, d_hbm, out_ref, xr, xh, xl, fv, gv, dv, scale, sv, s1,
           hrow, ecol, hcol, s2h, s2l, yv, mv, gsend, grecv, rsend, rrecv, hsend, hrecv, msem, lsem, ready):
    p, q = lax.axis_index("plane"), lax.axis_index("span")
    pair, half = p // 2, p % 2
    mine = q % 2
    col = half * 4 + q // 2
    row = pair * 2 + mine
    keeps = half == mine

    def worker(block_row, block_col):
        return block_row // 2 * 2 + block_col // 4, block_col % 4 * 2 + block_row % 2

    def inner(block, i):
        return jnp.where(block == 1, i, 3 - i)

    def rows(block, first, count):
        return pl.ds(jnp.where(block == 1, first, 4 - first - count), count)

    tables_in = [
        pltpu.make_async_copy(src, dst, lsem.at[i])
        for i, (src, dst) in enumerate(((f_hbm, fv), (g_hbm, gv), (d_hbm, dv)))
    ]
    for copy in tables_in:
        copy.start()

    first_ring = pair == 0
    late = first_ring & (half * 8 + q == 0)
    barrier = pltpu.get_barrier_semaphore()
    for i in range(1, 16):
        at = (half * 8 + q + i) % 16

        @pl.when(jnp.logical_not(late | (first_ring & (at == 0))))
        def _():
            pl.semaphore_signal(barrier, inc=1, device_id=(pair * 2 + at // 8, at % 8), device_id_type=MESH)

    outer = row + 2 * mine - 1
    has_outer = (outer >= 0) & (outer < planes)

    @pl.when(has_outer)
    def _():
        pl.semaphore_signal(barrier, inc=1, device_id=worker(outer, col), device_id_type=MESH)

    ring = jnp.where(first_ring & jnp.logical_not(late), 14, 15)
    pl.semaphore_wait(barrier, ring + jnp.where(has_outer, 1, 0))

    @pl.when(first_ring & jnp.logical_not(late))
    def _():
        pl.semaphore_signal(barrier, inc=1, device_id=(0, 0), device_id_type=MESH)

    @pl.when(late)
    def _():
        for at in range(1, 16):
            pl.semaphore_signal(ready, inc=1, device_id=(at // 8, at % 8), device_id_type=MESH)

    def gather(n, c, source, block):
        plane, span = worker(pair * 2 + half, c)
        part = rows(block, *IN[n])
        return pltpu.make_async_remote_copy(
            src_ref=x_ref.at[:, c, part], dst_ref=xr.at[source, :, part], send_sem=gsend.at[n, c],
            recv_sem=grecv.at[n, source], device_id=(plane, span), device_id_type=MESH)

    def gather_own(n):
        part = rows(half, *IN[n])
        return pltpu.make_async_copy(x_ref.at[:, col, part], xr.at[q, :, part], lsem.at[4 + n])

    def mask_own():
        return pltpu.make_async_copy(mask_ref.at[col], mv, lsem.at[3])

    def mask_sent():
        return pltpu.make_async_remote_copy(
            src_ref=mask_ref.at[(col + 4) % 8], dst_ref=mv, send_sem=msem.at[0], recv_sem=msem.at[1],
            device_id=(pair * 2 + 1 - half, q), device_id_type=MESH)

    @pl.when(keeps)
    def _():
        mask_own().start()
        mask_sent().start()

    def to_late(c):
        return first_ring & (half == 0) & (c == 0)

    def send_in(n):
        for d in (4, 3, 5, 2, 6, 1, 7, 0):
            c = (col + d) % 8
            held = to_late(c) if n < 2 else False
            if d == 0:
                @pl.when(keeps)
                def _():
                    gather_own(n).start()

                held |= keeps

            @pl.when(jnp.logical_not(held))
            def _():
                gather(n, c, q, half).start()

    send_in(0)
    send_in(1)

    @pl.when(first_ring & jnp.logical_not(late))
    def _():
        pl.semaphore_wait(ready, 1)

        @pl.when(half == 0)
        def _():
            gather(0, 0, q, half).start()
            gather(1, 0, q, half).start()

    for copy in tables_in:
        copy.wait()

    @pl.when(keeps)
    def _():
        mask_own().wait()

    @pl.when(jnp.logical_not(keeps))
    def _():
        mask_sent().wait_recv()

    for i in range(4):
        scale[i] = jnp.where(mv[inner(mine, i)] != 0, dv[1], dv[0])

    def receive(n):
        for i in range(8):
            own = keeps & (q == i)

            @pl.when(own)
            def _():
                gather_own(n).wait()

            @pl.when(jnp.logical_not(own))
            def _():
                gather(n, 0, i, mine).wait_recv()

            for at in range(IN[n][0], sum(IN[n])):
                high, low = split(xr[i, :, inner(mine, at), 0, :])
                xh[i * 64 : i * 64 + 64, at * 128 : at * 128 + 128] = high
                xl[i * 64 : i * 64 + 64, at * 128 : at * 128 + 128] = low

    def halo(i):
        if i < 2:
            to_row, to_col = row + (1 - 2 * mine if i == 0 else 2 * mine - 1), col
            src, dst = s1.at[3 * i], hrow.at[i]
            back = i
        else:
            to_row, to_col = row, col + 2 * (i % 2) - 1
            src, dst = ecol.at[i - 2], hcol.at[(i ^ 1) - 2]
            back = i ^ 1
        exists = (to_row >= 0) & (to_row < planes) & (to_col >= 0) & (to_col < 8)
        return exists, lambda: pltpu.make_async_remote_copy(
            src_ref=src, dst_ref=dst, send_sem=hsend.at[i], recv_sem=hrecv.at[back],
            device_id=worker(to_row, to_col), device_id_type=MESH)

    def send_halo(i):
        exists, copy = halo(i)

        @pl.when(exists)
        def _():
            copy().start()

    def take_halo(i):
        exists, _ = halo(i)
        dst = hrow.at[i] if i < 2 else hcol.at[i - 2]

        @pl.when(exists)
        def _():
            pltpu.make_async_remote_copy(
                src_ref=dst, dst_ref=dst, send_sem=hsend.at[i], recv_sem=hrecv.at[i],
                device_id=(p, q), device_id_type=MESH).wait_recv()

        @pl.when(jnp.logical_not(exists))
        def _():
            dst[...] = jnp.zeros(dst.shape, F32)

    lane = lax.broadcasted_iota(jnp.int32, (16, 128), 1)
    line = lax.broadcasted_iota(jnp.int32, (16, 128), 0)
    edge = jnp.where(line < 8, 0, 127)

    def pick(i):
        return jnp.where((line % 8 == i) & (lane == edge), 1.0, 0.0).astype(BF16)

    def lanes(i, count=1):
        return slice(i * 128, (i + count) * 128)

    def first_sweep(n):
        at = lanes(*IN[n])
        spectrum = dot(fv[0], xh[:, at]) + dot(fv[1], xh[:, at]) + dot(fv[0], xl[:, at])
        edges = jnp.zeros((16, MODES), F32)
        for j in range(IN[n][1]):
            i = IN[n][0] + j
            part = spectrum[:, lanes(j)]
            sv[:, lanes(i)] = part
            part = part * scale[i]
            s1[i] = part
            if i % 3 == 0:
                send_halo(i // 3)
            for piece in split(part):
                edges += lax.dot_general(pick(i), piece, (((1,), (1,)), ((), ())), preferred_element_type=F32)
        ecol[2 * n] = edges[:8]
        ecol[2 * n + 1] = edges[8:]
        send_halo(2 + 2 * n)
        send_halo(3 + 2 * n)

    wide = lax.broadcasted_iota(jnp.int32, (MODES, 128), 1)

    def columns(n):
        take_halo(2 + 2 * n)
        take_halo(3 + 2 * n)
        return split(jnp.concatenate([hcol[2 * n], hcol[2 * n + 1]], axis=0).T)

    def own_terms(i):
        here = s1[i]
        total = sv[:, lanes(i)]
        total += jnp.where(wide == 0, 0.0, pltpu.roll(here, 1, 1))
        total += jnp.where(wide == 127, 0.0, pltpu.roll(here, 127, 1))
        if i > 0:
            total += s1[i - 1]
        if i < 3:
            total += s1[i + 1]
        sv[:, lanes(i)] = total

    def second_sweep(i, sides):
        total = sv[:, lanes(i)]
        if i % 3 == 0:
            total += hrow[i // 3]
        for piece in sides:
            total += dot(piece, pick(i))
        high, low = split(total * scale[i])
        s2h[:, lanes(i)] = high
        s2l[:, lanes(i)] = low

    def scatter(n, target, c, block):
        part = rows(block, *OUT[n])
        return pltpu.make_async_remote_copy(
            src_ref=yv.at[target, :, part], dst_ref=out_ref.at[:, c, part], send_sem=rsend.at[n, target],
            recv_sem=rrecv.at[n, c], device_id=(pair * 2 + mine, target), device_id_type=MESH)

    def scatter_own(n):
        part = rows(mine, *OUT[n])
        return pltpu.make_async_copy(yv.at[q, :, part], out_ref.at[:, col, part], lsem.at[7 + n])

    first = q // 2 + jnp.where(keeps, 2, 0)

    def start_scatter(n, target):
        own = keeps & (target == q)

        @pl.when(own)
        def _():
            scatter_own(n).start()

        @pl.when(jnp.logical_not(own))
        def _():
            scatter(n, target, col, mine).start()

    def inverse(h, n):
        at = lanes(2 * h, 2)
        for k in range(4):
            j = (first + k) % 4
            cells = pl.ds(pl.multiple_of(j * 128, 128), 128)
            field = dot(gv[0, cells, :], s2h[:, at]) + dot(gv[1, cells, :], s2h[:, at]) + dot(gv[0, cells, :], s2l[:, at])
            for core in range(2):
                target = j * 2 + core
                for i in range(2):
                    yv[target, :, inner(mine, 2 * h + i), 0, :] = field[core * 64 : core * 64 + 64, lanes(i)]
                start_scatter(n, target)

    receive(0)
    first_sweep(0)
    send_in(2)
    own_terms(0)
    receive(1)
    first_sweep(1)
    own_terms(1)
    sides = columns(0)
    take_halo(0)
    second_sweep(0, sides)
    second_sweep(1, sides)
    inverse(0, 0)
    receive(2)
    first_sweep(2)
    for k in range(4):
        for core in range(2):
            start_scatter(1, (first + k) % 4 * 2 + core)
    own_terms(2)
    own_terms(3)
    second_sweep(2, columns(1))
    sides = columns(2)
    take_halo(1)
    second_sweep(3, sides)
    inverse(1, 2)

    for n in range(3):
        for c in range(8):
            own = keeps & (c == col)

            @pl.when(own)
            def _():
                scatter_own(n).wait()

            @pl.when(jnp.logical_not(own))
            def _():
                scatter(n, 0, c, half).wait_recv()

        for target in range(8):
            @pl.when(jnp.logical_not(keeps & (target == q)))
            def _():
                scatter(n, target, col, mine).wait_send()

    for c in range(8):
        @pl.when(jnp.logical_not(keeps & (c == col)))
        def _():
            for n in range(3):
                gather(n, c, q, half).wait_send()

    for i in range(8):
        exists, copy = halo(i)

        @pl.when(exists)
        def _():
            copy().wait_send()

    @pl.when(keeps)
    def _():
        mask_sent().wait_send()


def local(planes, consts, pressure_source, solid_mask):
    anywhere = pl.BlockSpec(memory_space=pl.ANY)
    dma = pltpu.SemaphoreType.DMA
    source = pressure_source.reshape(64, 4, 8, 128).transpose(0, 2, 1, 3).reshape(64, 8, 4, 1, 128)
    mask = solid_mask.reshape(4, 8, 128).transpose(1, 0, 2).reshape(8, 4, 1, 128)
    out = pl.pallas_call(
        functools.partial(kernel, planes),
        out_shape=pltpu.VMEM(source.shape, F32),
        in_specs=[anywhere] * 5,
        out_specs=anywhere,
        scratch_shapes=[
            pltpu.VMEM((8, 64, 4, 1, 128), F32),
            pltpu.VMEM((NS, 512), BF16),
            pltpu.VMEM((NS, 512), BF16),
            pltpu.VMEM((2, MODES, NS), BF16),
            pltpu.VMEM((2, NS, MODES), BF16),
            pltpu.VMEM((2, MODES, 128), F32),
            pltpu.VMEM((4, MODES, 128), F32),
            pltpu.VMEM((MODES, 512), F32),
            pltpu.VMEM((4, MODES, 128), F32),
            pltpu.VMEM((2, MODES, 128), F32),
            pltpu.VMEM((6, 8, MODES), F32),
            pltpu.VMEM((6, 8, MODES), F32),
            pltpu.VMEM((MODES, 512), BF16),
            pltpu.VMEM((MODES, 512), BF16),
            pltpu.VMEM((8, 64, 4, 1, 128), F32),
            pltpu.VMEM((4, 1, 128), jnp.int32),
            dma((3, 8)), dma((3, 8)), dma((3, 8)), dma((3, 8)), dma((8,)), dma((8,)), dma((2,)), dma((10,)),
            pltpu.SemaphoreType.REGULAR,
        ],
        compiler_params=pltpu.CompilerParams(
            collective_id=0, has_side_effects=True, vmem_limit_bytes=40 * 1024 * 1024),
    )(*[pltpu.with_memory_space_constraint(v, pltpu.HBM) for v in (source, mask, *consts)])
    def copy_out(src, dst, sem):
        copy = pltpu.make_async_copy(src, dst, sem)
        copy.start()
        copy.wait()

    out = pl.pallas_call(
        copy_out, out_shape=pltpu.HBM(source.shape, F32), in_specs=[pl.BlockSpec(memory_space=pltpu.VMEM)], out_specs=anywhere,
        scratch_shapes=[dma(())])(pltpu.with_memory_space_constraint(out, pltpu.VMEM))
    return out.reshape(64, 8, 4, 128).transpose(0, 2, 1, 3).reshape(64, 4, 1024)


def solution(mesh):
    consts = tables()

    def step(pressure_source, solid_mask):
        return local(mesh.shape["plane"], [jnp.asarray(c) for c in consts], pressure_source, solid_mask)

    return jax.shard_map(
        step, mesh=mesh, in_specs=(P("span", "plane", None), P("plane", None)),
        out_specs=P("span", "plane", None), check_vma=False)
```

```python
import functools

import jax
import jax.numpy as jnp
import ml_dtypes
import numpy as np
from jax import lax
from jax.experimental import pallas as pl
from jax.experimental.pallas import tpu as pltpu
from jax.sharding import PartitionSpec as P

MESH = pl.DeviceIdType.MESH
NS = 512
MODES = 352
PENALTY = 12.0
IN = ((0, 2), (2, 1), (3, 1))
OUT = ((0, 1), (1, 1), (2, 2))
F32, BF16 = jnp.float32, jnp.bfloat16


def tables():
    modes = np.arange(NS)
    wave = np.where(modes <= NS // 2, modes, modes - NS // 2)
    kept = np.nonzero(3 * wave <= NS)[0]
    wave, cosine = wave[kept], kept <= NS // 2
    angle = (np.arange(NS)[None, :] * wave[:, None] % NS) * (2.0 * np.pi / NS)
    forward = np.zeros((MODES, NS))
    forward[: len(kept)] = np.where(cosine[:, None], np.cos(angle), np.sin(angle))
    weight = np.where(cosine & ((wave == 0) | (wave == NS // 2)), 1.0, 2.0) / NS
    inverse = np.zeros((NS, MODES))
    inverse[:, : len(kept)] = (forward[: len(kept)] * weight[:, None]).T
    eigen = np.zeros(MODES)
    eigen[: len(kept)] = 2.0 - 2.0 * np.cos(wave * (2.0 * np.pi / NS))
    scale = np.stack([1.0 / (4.0 + eigen), 1.0 / (4.0 + eigen + PENALTY)])
    scale = np.broadcast_to(scale[:, :, None], (2, MODES, 128))

    def halves(x):
        high = x.astype(ml_dtypes.bfloat16)
        return np.stack([high, (x - high.astype(np.float64)).astype(ml_dtypes.bfloat16)])

    return halves(forward), halves(inverse), np.ascontiguousarray(scale, dtype=np.float32)


def split(x):
    high = x.astype(BF16)
    return high, (x - high.astype(F32)).astype(BF16)


def dot(a, b):
    return jnp.dot(a, b, preferred_element_type=F32)


def kernel(planes, x_ref, mask_ref, f_hbm, g_hbm, d_hbm, out_ref, xr, xh, xl, fv, gv, dv, scale, sv, s1,
           hrow, ecol, hcol, s2h, s2l, yv, mv, gsend, grecv, rsend, rrecv, hsend, hrecv, msem, lsem, ready):
    p, q = lax.axis_index("plane"), lax.axis_index("span")
    pair, half = p // 2, p % 2
    mine = q % 2
    col = half * 4 + q // 2
    row = pair * 2 + mine
    keeps = half == mine

    def worker(block_row, block_col):
        return block_row // 2 * 2 + block_col // 4, block_col % 4 * 2 + block_row % 2

    def inner(block, i):
        return jnp.where(block == 1, i, 3 - i)

    def rows(block, first, count):
        return pl.ds(jnp.where(block == 1, first, 4 - first - count), count)

    first_ring = pair == 0
    late = first_ring & (half * 8 + q == 0)
    barrier = pltpu.get_barrier_semaphore()
    for i in range(1, 16):
        at = (half * 8 + q + i) % 16

        @pl.when(jnp.logical_not(late | (first_ring & (at == 0))))
        def _():
            pl.semaphore_signal(barrier, inc=1, device_id=(pair * 2 + at // 8, at % 8), device_id_type=MESH)

    outer = row + 2 * mine - 1
    has_outer = (outer >= 0) & (outer < planes)

    @pl.when(has_outer)
    def _():
        pl.semaphore_signal(barrier, inc=1, device_id=worker(outer, col), device_id_type=MESH)

    tables_in = [
        pltpu.make_async_copy(src, dst, lsem.at[i])
        for i, (src, dst) in enumerate(((f_hbm, fv), (g_hbm, gv), (d_hbm, dv)))
    ]
    for copy in tables_in:
        copy.start()

    ring = jnp.where(first_ring & jnp.logical_not(late), 14, 15)
    pl.semaphore_wait(barrier, ring + jnp.where(has_outer, 1, 0))

    @pl.when(first_ring & jnp.logical_not(late))
    def _():
        pl.semaphore_signal(barrier, inc=1, device_id=(0, 0), device_id_type=MESH)

    @pl.when(late)
    def _():
        for at in range(1, 16):
            pl.semaphore_signal(ready, inc=1, device_id=(at // 8, at % 8), device_id_type=MESH)

    def gather(n, c, source, block):
        plane, span = worker(pair * 2 + half, c)
        part = rows(block, *IN[n])
        return pltpu.make_async_remote_copy(
            src_ref=x_ref.at[:, c, part], dst_ref=xr.at[source, :, part], send_sem=gsend.at[n, c],
            recv_sem=grecv.at[n, source], device_id=(plane, span), device_id_type=MESH)

    def gather_own(n):
        part = rows(half, *IN[n])
        return pltpu.make_async_copy(x_ref.at[:, col, part], xr.at[q, :, part], lsem.at[4 + n])

    def mask_own():
        return pltpu.make_async_copy(mask_ref.at[col], mv, lsem.at[3])

    def mask_sent():
        return pltpu.make_async_remote_copy(
            src_ref=mask_ref.at[(col + 4) % 8], dst_ref=mv, send_sem=msem.at[0], recv_sem=msem.at[1],
            device_id=(pair * 2 + 1 - half, q), device_id_type=MESH)

    @pl.when(keeps)
    def _():
        mask_own().start()
        mask_sent().start()

    def to_late(c):
        return first_ring & (half == 0) & (c == 0)

    def send_in(n):
        for d in (4, 3, 5, 2, 6, 1, 7, 0):
            c = (col + d) % 8
            held = to_late(c)
            if d == 0:
                @pl.when(keeps)
                def _():
                    gather_own(n).start()

                held |= keeps

            @pl.when(jnp.logical_not(held))
            def _():
                gather(n, c, q, half).start()

    send_in(0)
    send_in(1)

    @pl.when(first_ring & jnp.logical_not(late))
    def _():
        pl.semaphore_wait(ready, 1)

        @pl.when(half == 0)
        def _():
            for n in range(3):
                gather(n, 0, q, half).start()

    @pl.when(late)
    def _():
        send_in(2)

    for copy in tables_in:
        copy.wait()

    @pl.when(keeps)
    def _():
        mask_own().wait()

    @pl.when(jnp.logical_not(keeps))
    def _():
        mask_sent().wait_recv()

    for i in range(4):
        scale[i] = jnp.where(mv[inner(mine, i)] != 0, dv[1], dv[0])

    def receive(n):
        for i in range(8):
            own = keeps & (q == i)

            @pl.when(own)
            def _():
                gather_own(n).wait()

            @pl.when(jnp.logical_not(own))
            def _():
                gather(n, 0, i, mine).wait_recv()

            for at in range(IN[n][0], sum(IN[n])):
                high, low = split(xr[i, :, inner(mine, at), 0, :])
                xh[i * 64 : i * 64 + 64, at * 128 : at * 128 + 128] = high
                xl[i * 64 : i * 64 + 64, at * 128 : at * 128 + 128] = low

    def halo(i):
        if i < 2:
            to_row, to_col = row + (1 - 2 * mine if i == 0 else 2 * mine - 1), col
            src, dst = s1.at[3 * i], hrow.at[i]
            back = i
        else:
            to_row, to_col = row, col + 2 * (i % 2) - 1
            src, dst = ecol.at[i - 2], hcol.at[(i ^ 1) - 2]
            back = i ^ 1
        exists = (to_row >= 0) & (to_row < planes) & (to_col >= 0) & (to_col < 8)
        return exists, lambda: pltpu.make_async_remote_copy(
            src_ref=src, dst_ref=dst, send_sem=hsend.at[i], recv_sem=hrecv.at[back],
            device_id=worker(to_row, to_col), device_id_type=MESH)

    def send_halo(i):
        exists, copy = halo(i)

        @pl.when(exists)
        def _():
            copy().start()

    def take_halo(i):
        exists, _ = halo(i)
        dst = hrow.at[i] if i < 2 else hcol.at[i - 2]

        @pl.when(exists)
        def _():
            pltpu.make_async_remote_copy(
                src_ref=dst, dst_ref=dst, send_sem=hsend.at[i], recv_sem=hrecv.at[i],
                device_id=(p, q), device_id_type=MESH).wait_recv()

        @pl.when(jnp.logical_not(exists))
        def _():
            dst[...] = jnp.zeros(dst.shape, F32)

    lane = lax.broadcasted_iota(jnp.int32, (16, 128), 1)
    line = lax.broadcasted_iota(jnp.int32, (16, 128), 0)
    edge = jnp.where(line < 8, 0, 127)

    def pick(i):
        return jnp.where((line % 8 == i) & (lane == edge), 1.0, 0.0).astype(BF16)

    def lanes(i, count=1):
        return slice(i * 128, (i + count) * 128)

    def first_sweep(n):
        at = lanes(*IN[n])
        spectrum = dot(fv[0], xh[:, at]) + dot(fv[1], xh[:, at]) + dot(fv[0], xl[:, at])
        edges = jnp.zeros((16, MODES), F32)
        for j in range(IN[n][1]):
            i = IN[n][0] + j
            part = spectrum[:, lanes(j)]
            sv[:, lanes(i)] = part
            part = part * scale[i]
            s1[i] = part
            if i % 3 == 0:
                send_halo(i // 3)
            for piece in split(part):
                edges += lax.dot_general(pick(i), piece, (((1,), (1,)), ((), ())), preferred_element_type=F32)
        ecol[2 * n] = edges[:8]
        ecol[2 * n + 1] = edges[8:]
        send_halo(2 + 2 * n)
        send_halo(3 + 2 * n)

    wide = lax.broadcasted_iota(jnp.int32, (MODES, 128), 1)

    def columns(n):
        take_halo(2 + 2 * n)
        take_halo(3 + 2 * n)
        return split(jnp.concatenate([hcol[2 * n], hcol[2 * n + 1]], axis=0).T)

    def own_terms(i):
        here = s1[i]
        total = sv[:, lanes(i)]
        total += jnp.where(wide == 0, 0.0, pltpu.roll(here, 1, 1))
        total += jnp.where(wide == 127, 0.0, pltpu.roll(here, 127, 1))
        if i > 0:
            total += s1[i - 1]
        if i < 3:
            total += s1[i + 1]
        sv[:, lanes(i)] = total

    def second_sweep(i, sides):
        total = sv[:, lanes(i)]
        if i % 3 == 0:
            total += hrow[i // 3]
        for piece in sides:
            total += dot(piece, pick(i))
        high, low = split(total * scale[i])
        s2h[:, lanes(i)] = high
        s2l[:, lanes(i)] = low

    def scatter(n, target, c, block):
        part = rows(block, *OUT[n])
        return pltpu.make_async_remote_copy(
            src_ref=yv.at[target, :, part], dst_ref=out_ref.at[:, c, part], send_sem=rsend.at[n, target],
            recv_sem=rrecv.at[n, c], device_id=(pair * 2 + mine, target), device_id_type=MESH)

    def scatter_own(n):
        part = rows(mine, *OUT[n])
        return pltpu.make_async_copy(yv.at[q, :, part], out_ref.at[:, col, part], lsem.at[7 + n])

    def chip(k):
        return (q // 2 + jnp.where(keeps, (2, 3, 1, 0)[k], (0, 3, 1, 2)[k])) % 4


    def start_scatter(n, target):
        own = keeps & (target == q)

        @pl.when(own)
        def _():
            scatter_own(n).start()

        @pl.when(jnp.logical_not(own))
        def _():
            scatter(n, target, col, mine).start()

    def inverse(h, n):
        at = lanes(2 * h, 2)
        for k in range(4):
            j = chip(k)
            cells = pl.ds(pl.multiple_of(j * 128, 128), 128)
            field = dot(gv[0, cells, :], s2h[:, at]) + dot(gv[1, cells, :], s2h[:, at]) + dot(gv[0, cells, :], s2l[:, at])
            for core in range(2):
                target = j * 2 + core
                for i in range(2):
                    yv[target, :, inner(mine, 2 * h + i), 0, :] = field[core * 64 : core * 64 + 64, lanes(i)]
                start_scatter(n, target)

    receive(0)
    first_sweep(0)

    @pl.when(jnp.logical_not(late))
    def _():
        send_in(2)

    own_terms(0)
    receive(1)
    first_sweep(1)
    own_terms(1)
    sides = columns(0)
    take_halo(0)
    second_sweep(0, sides)
    second_sweep(1, sides)
    inverse(0, 0)
    receive(2)
    first_sweep(2)
    for k in range(4):
        for core in range(2):
            start_scatter(1, chip(k) * 2 + core)
    own_terms(2)
    own_terms(3)
    second_sweep(2, columns(1))
    sides = columns(2)
    take_halo(1)
    second_sweep(3, sides)
    inverse(1, 2)

    for n in range(3):
        for c in range(8):
            own = keeps & (c == col)

            @pl.when(own)
            def _():
                scatter_own(n).wait()

            @pl.when(jnp.logical_not(own))
            def _():
                scatter(n, 0, c, half).wait_recv()

        for target in range(8):
            @pl.when(jnp.logical_not(keeps & (target == q)))
            def _():
                scatter(n, target, col, mine).wait_send()

    for c in range(8):
        @pl.when(jnp.logical_not(keeps & (c == col)))
        def _():
            for n in range(3):
                gather(n, c, q, half).wait_send()

    for i in range(8):
        exists, copy = halo(i)

        @pl.when(exists)
        def _():
            copy().wait_send()

    @pl.when(keeps)
    def _():
        mask_sent().wait_send()


def local(planes, consts, pressure_source, solid_mask):
    anywhere = pl.BlockSpec(memory_space=pl.ANY)
    dma = pltpu.SemaphoreType.DMA
    source = pressure_source.reshape(64, 4, 8, 128).transpose(0, 2, 1, 3).reshape(64, 8, 4, 1, 128)
    mask = solid_mask.reshape(4, 8, 128).transpose(1, 0, 2).reshape(8, 4, 1, 128)
    out = pl.pallas_call(
        functools.partial(kernel, planes),
        out_shape=pltpu.VMEM(source.shape, F32),
        in_specs=[anywhere] * 5,
        out_specs=anywhere,
        scratch_shapes=[
            pltpu.VMEM((8, 64, 4, 1, 128), F32),
            pltpu.VMEM((NS, 512), BF16),
            pltpu.VMEM((NS, 512), BF16),
            pltpu.VMEM((2, MODES, NS), BF16),
            pltpu.VMEM((2, NS, MODES), BF16),
            pltpu.VMEM((2, MODES, 128), F32),
            pltpu.VMEM((4, MODES, 128), F32),
            pltpu.VMEM((MODES, 512), F32),
            pltpu.VMEM((4, MODES, 128), F32),
            pltpu.VMEM((2, MODES, 128), F32),
            pltpu.VMEM((6, 8, MODES), F32),
            pltpu.VMEM((6, 8, MODES), F32),
            pltpu.VMEM((MODES, 512), BF16),
            pltpu.VMEM((MODES, 512), BF16),
            pltpu.VMEM((8, 64, 4, 1, 128), F32),
            pltpu.VMEM((4, 1, 128), jnp.int32),
            dma((3, 8)), dma((3, 8)), dma((3, 8)), dma((3, 8)), dma((8,)), dma((8,)), dma((2,)), dma((10,)),
            pltpu.SemaphoreType.REGULAR,
        ],
        compiler_params=pltpu.CompilerParams(
            collective_id=0, has_side_effects=True, vmem_limit_bytes=40 * 1024 * 1024),
    )(*[pltpu.with_memory_space_constraint(v, pltpu.HBM) for v in (source, mask, *consts)])
    def copy_out(src, dst, sem):
        copies = [pltpu.make_async_copy(src.at[pl.ds(8 * i, 8)], dst.at[pl.ds(8 * i, 8)], sem.at[i]) for i in range(8)]
        for copy in copies:
            copy.start()
        for copy in copies:
            copy.wait()

    out = pl.pallas_call(
        copy_out, out_shape=pltpu.HBM(source.shape, F32), in_specs=[pl.BlockSpec(memory_space=pltpu.VMEM)], out_specs=anywhere,
        scratch_shapes=[dma((8,))])(pltpu.with_memory_space_constraint(out, pltpu.VMEM))
    return out.reshape(64, 8, 4, 128).transpose(0, 2, 1, 3).reshape(64, 4, 1024)


def solution(mesh):
    consts = tables()

    def step(pressure_source, solid_mask):
        return local(mesh.shape["plane"], [jnp.asarray(c) for c in consts], pressure_source, solid_mask)

    return jax.shard_map(
        step, mesh=mesh, in_specs=(P("span", "plane", None), P("plane", None)),
        out_specs=P("span", "plane", None), check_vma=False)
```

```python
import functools

import jax
import jax.numpy as jnp
import ml_dtypes
import numpy as np
from jax import lax
from jax.experimental import pallas as pl
from jax.experimental.pallas import tpu as pltpu
from jax.sharding import PartitionSpec as P

MESH = pl.DeviceIdType.MESH
NS = 512
MODES = 352
PENALTY = 12.0
IN = ((0, 2), (2, 1), (3, 1))
OUT = ((0, 1), (1, 1), (2, 2))
F32, BF16 = jnp.float32, jnp.bfloat16


def tables():
    modes = np.arange(NS)
    wave = np.where(modes <= NS // 2, modes, modes - NS // 2)
    kept = np.nonzero(3 * wave <= NS)[0]
    wave, cosine = wave[kept], kept <= NS // 2
    angle = (np.arange(NS)[None, :] * wave[:, None] % NS) * (2.0 * np.pi / NS)
    forward = np.zeros((MODES, NS))
    forward[: len(kept)] = np.where(cosine[:, None], np.cos(angle), np.sin(angle))
    weight = np.where(cosine & ((wave == 0) | (wave == NS // 2)), 1.0, 2.0) / NS
    inverse = np.zeros((NS, MODES))
    inverse[:, : len(kept)] = (forward[: len(kept)] * weight[:, None]).T
    eigen = np.zeros(MODES)
    eigen[: len(kept)] = 2.0 - 2.0 * np.cos(wave * (2.0 * np.pi / NS))
    scale = np.stack([1.0 / (4.0 + eigen), 1.0 / (4.0 + eigen + PENALTY)])
    scale = np.broadcast_to(scale[:, :, None], (2, MODES, 128))

    def halves(x):
        high = x.astype(ml_dtypes.bfloat16)
        return np.stack([high, (x - high.astype(np.float64)).astype(ml_dtypes.bfloat16)])

    return halves(forward), halves(inverse), np.ascontiguousarray(scale, dtype=np.float32)


def split(x):
    high = x.astype(BF16)
    return high, (x - high.astype(F32)).astype(BF16)


def dot(a, b):
    return jnp.dot(a, b, preferred_element_type=F32)


def kernel(planes, x_ref, mask_ref, f_hbm, g_hbm, d_hbm, out_ref, xr, xh, xl, fv, gv, dv, scale, sv, s1,
           hrow, ecol, hcol, s2h, s2l, yv, mv, gsend, grecv, rsend, rrecv, hsend, hrecv, msem, lsem, ready):
    p, q = lax.axis_index("plane"), lax.axis_index("span")
    pair, half = p // 2, p % 2
    mine = q % 2
    col = half * 4 + q // 2
    row = pair * 2 + mine
    keeps = half == mine

    def worker(block_row, block_col):
        return block_row // 2 * 2 + block_col // 4, block_col % 4 * 2 + block_row % 2

    def inner(block, i):
        return jnp.where(block == 1, i, 3 - i)

    def rows(block, first, count):
        return pl.ds(jnp.where(block == 1, first, 4 - first - count), count)

    first_ring = pair == 0
    late = first_ring & (half * 8 + q == 0)
    barrier = pltpu.get_barrier_semaphore()
    def greet(i):
        at = (half * 8 + q + i) % 16
        pl.semaphore_signal(barrier, inc=1, device_id=(pair * 2 + at // 8, at % 8), device_id_type=MESH)

    @pl.when(jnp.logical_not(first_ring))
    def _():
        for i in range(1, 16):
            greet(i)

    @pl.when(first_ring & jnp.logical_not(late))
    def _():
        for i in range(1, 16):
            @pl.when((half * 8 + q + i) % 16 != 0)
            def _():
                greet(i)

    outer = row + 2 * mine - 1
    has_outer = (outer >= 0) & (outer < planes)

    @pl.when(has_outer)
    def _():
        pl.semaphore_signal(barrier, inc=1, device_id=worker(outer, col), device_id_type=MESH)

    tables_in = [
        pltpu.make_async_copy(src, dst, lsem.at[i])
        for i, (src, dst) in enumerate(((f_hbm, fv), (g_hbm, gv), (d_hbm, dv)))
    ]
    for copy in tables_in:
        copy.start()

    ring = jnp.where(first_ring & jnp.logical_not(late), 14, 15)
    pl.semaphore_wait(barrier, ring + jnp.where(has_outer, 1, 0))

    @pl.when(first_ring & jnp.logical_not(late))
    def _():
        pl.semaphore_signal(barrier, inc=1, device_id=(0, 0), device_id_type=MESH)

    @pl.when(late)
    def _():
        for at in range(1, 16):
            pl.semaphore_signal(ready, inc=1, device_id=(at // 8, at % 8), device_id_type=MESH)

    def gather(n, c, source, block):
        plane, span = worker(pair * 2 + half, c)
        part = rows(block, *IN[n])
        return pltpu.make_async_remote_copy(
            src_ref=x_ref.at[:, c, part], dst_ref=xr.at[source, :, part], send_sem=gsend.at[n, c],
            recv_sem=grecv.at[n, source], device_id=(plane, span), device_id_type=MESH)

    def gather_own(n):
        part = rows(half, *IN[n])
        return pltpu.make_async_copy(x_ref.at[:, col, part], xr.at[q, :, part], lsem.at[4 + n])

    def mask_own():
        return pltpu.make_async_copy(mask_ref.at[col], mv, lsem.at[3])

    def mask_sent():
        return pltpu.make_async_remote_copy(
            src_ref=mask_ref.at[(col + 4) % 8], dst_ref=mv, send_sem=msem.at[0], recv_sem=msem.at[1],
            device_id=(pair * 2 + 1 - half, q), device_id_type=MESH)

    @pl.when(keeps)
    def _():
        mask_own().start()
        mask_sent().start()

    def to_late(c):
        return first_ring & (half == 0) & (c == 0)

    def send_in(n):
        for d in (4, 5, 3, 6, 2, 7, 1, 0):
            c = (col + d) % 8
            held = to_late(c)
            if d == 0:
                @pl.when(keeps)
                def _():
                    gather_own(n).start()

                held |= keeps

            @pl.when(jnp.logical_not(held))
            def _():
                gather(n, c, q, half).start()

    send_in(0)
    send_in(1)

    @pl.when(first_ring & jnp.logical_not(late))
    def _():
        pl.semaphore_wait(ready, 1)

        @pl.when(half == 0)
        def _():
            for n in range(3):
                gather(n, 0, q, half).start()

    @pl.when(late)
    def _():
        send_in(2)

    for copy in tables_in:
        copy.wait()

    @pl.when(keeps)
    def _():
        mask_own().wait()

    @pl.when(jnp.logical_not(keeps))
    def _():
        mask_sent().wait_recv()

    for i in range(4):
        scale[i] = jnp.where(mv[inner(mine, i)] != 0, dv[1], dv[0])

    def receive(n):
        for i in range(8):
            own = keeps & (q == i)

            @pl.when(own)
            def _():
                gather_own(n).wait()

            @pl.when(jnp.logical_not(own))
            def _():
                gather(n, 0, i, mine).wait_recv()

            for at in range(IN[n][0], sum(IN[n])):
                high, low = split(xr[i, :, inner(mine, at), 0, :])
                xh[i * 64 : i * 64 + 64, at * 128 : at * 128 + 128] = high
                xl[i * 64 : i * 64 + 64, at * 128 : at * 128 + 128] = low

    def halo(i):
        if i < 2:
            to_row, to_col = row + (1 - 2 * mine if i == 0 else 2 * mine - 1), col
            src, dst = s1.at[3 * i], hrow.at[i]
            back = i
        else:
            to_row, to_col = row, col + 2 * (i % 2) - 1
            src, dst = ecol.at[i - 2], hcol.at[(i ^ 1) - 2]
            back = i ^ 1
        exists = (to_row >= 0) & (to_row < planes) & (to_col >= 0) & (to_col < 8)
        return exists, lambda: pltpu.make_async_remote_copy(
            src_ref=src, dst_ref=dst, send_sem=hsend.at[i], recv_sem=hrecv.at[back],
            device_id=worker(to_row, to_col), device_id_type=MESH)

    def send_halo(i):
        exists, copy = halo(i)

        @pl.when(exists)
        def _():
            copy().start()

    def take_halo(i):
        exists, _ = halo(i)
        dst = hrow.at[i] if i < 2 else hcol.at[i - 2]

        @pl.when(exists)
        def _():
            pltpu.make_async_remote_copy(
                src_ref=dst, dst_ref=dst, send_sem=hsend.at[i], recv_sem=hrecv.at[i],
                device_id=(p, q), device_id_type=MESH).wait_recv()

        @pl.when(jnp.logical_not(exists))
        def _():
            dst[...] = jnp.zeros(dst.shape, F32)

    lane = lax.broadcasted_iota(jnp.int32, (16, 128), 1)
    line = lax.broadcasted_iota(jnp.int32, (16, 128), 0)
    edge = jnp.where(line < 8, 0, 127)

    def pick(i):
        return jnp.where((line % 8 == i) & (lane == edge), 1.0, 0.0).astype(BF16)

    def lanes(i, count=1):
        return slice(i * 128, (i + count) * 128)

    def first_sweep(n):
        at = lanes(*IN[n])
        spectrum = dot(fv[0], xh[:, at]) + dot(fv[1], xh[:, at]) + dot(fv[0], xl[:, at])
        edges = jnp.zeros((16, MODES), F32)
        for j in range(IN[n][1]):
            i = IN[n][0] + j
            part = spectrum[:, lanes(j)]
            sv[:, lanes(i)] = part
            part = part * scale[i]
            s1[i] = part
            if i % 3 == 0:
                send_halo(i // 3)
            for piece in split(part):
                edges += lax.dot_general(pick(i), piece, (((1,), (1,)), ((), ())), preferred_element_type=F32)
        ecol[2 * n] = edges[:8]
        ecol[2 * n + 1] = edges[8:]
        send_halo(2 + 2 * n)
        send_halo(3 + 2 * n)

    wide = lax.broadcasted_iota(jnp.int32, (MODES, 128), 1)

    def columns(n):
        take_halo(2 + 2 * n)
        take_halo(3 + 2 * n)
        return split(jnp.concatenate([hcol[2 * n], hcol[2 * n + 1]], axis=0).T)

    def own_terms(i):
        here = s1[i]
        total = sv[:, lanes(i)]
        total += jnp.where(wide == 0, 0.0, pltpu.roll(here, 1, 1))
        total += jnp.where(wide == 127, 0.0, pltpu.roll(here, 127, 1))
        if i > 0:
            total += s1[i - 1]
        if i < 3:
            total += s1[i + 1]
        sv[:, lanes(i)] = total

    def second_sweep(i, sides):
        total = sv[:, lanes(i)]
        if i % 3 == 0:
            total += hrow[i // 3]
        for piece in sides:
            total += dot(piece, pick(i))
        high, low = split(total * scale[i])
        s2h[:, lanes(i)] = high
        s2l[:, lanes(i)] = low

    def scatter(n, target, c, block):
        part = rows(block, *OUT[n])
        return pltpu.make_async_remote_copy(
            src_ref=yv.at[target, :, part], dst_ref=out_ref.at[:, c, part], send_sem=rsend.at[n, target],
            recv_sem=rrecv.at[n, c], device_id=(pair * 2 + mine, target), device_id_type=MESH)

    def scatter_own(n):
        part = rows(mine, *OUT[n])
        return pltpu.make_async_copy(yv.at[q, :, part], out_ref.at[:, col, part], lsem.at[7 + n])

    def chip(k):
        return (q // 2 + jnp.where(keeps, (2, 3, 1, 0)[k], (0, 3, 1, 2)[k])) % 4


    def start_scatter(n, target):
        own = keeps & (target == q)

        @pl.when(own)
        def _():
            scatter_own(n).start()

        @pl.when(jnp.logical_not(own))
        def _():
            scatter(n, target, col, mine).start()

    def inverse(h, n):
        at = lanes(2 * h, 2)
        for k in range(4):
            j = chip(k)
            cells = pl.ds(pl.multiple_of(j * 128, 128), 128)
            field = dot(gv[0, cells, :], s2h[:, at]) + dot(gv[1, cells, :], s2h[:, at]) + dot(gv[0, cells, :], s2l[:, at])
            for core in range(2):
                target = j * 2 + core
                for i in range(2):
                    yv[target, :, inner(mine, 2 * h + i), 0, :] = field[core * 64 : core * 64 + 64, lanes(i)]
                start_scatter(n, target)

    receive(0)
    first_sweep(0)

    @pl.when(jnp.logical_not(late))
    def _():
        send_in(2)

    own_terms(0)
    receive(1)
    first_sweep(1)
    own_terms(1)
    sides = columns(0)
    take_halo(0)
    second_sweep(0, sides)
    second_sweep(1, sides)
    inverse(0, 0)
    receive(2)
    first_sweep(2)
    for k in range(4):
        for core in range(2):
            start_scatter(1, chip(k) * 2 + core)
    own_terms(2)
    own_terms(3)
    second_sweep(2, columns(1))
    sides = columns(2)
    take_halo(1)
    second_sweep(3, sides)
    inverse(1, 2)

    for d in range(8):
        c = (col + d) % 8

        @pl.when(jnp.logical_not(keeps & (d == 0)))
        def _():
            for n in range(3):
                gather(n, c, q, half).wait_send()

    for i in range(8):
        exists, copy = halo(i)

        @pl.when(exists)
        def _():
            copy().wait_send()

    @pl.when(keeps)
    def _():
        mask_sent().wait_send()

    for n in range(3):
        @pl.when(keeps)
        def _():
            scatter_own(n).wait()

        for i in range(8):
            @pl.when(jnp.logical_not(keeps & (i == 0)))
            def _():
                scatter(n, (q + i) % 8, col, mine).wait_send()

        for d in range(8):
            @pl.when(jnp.logical_not(keeps & (d == 0)))
            def _():
                scatter(n, 0, (col + d) % 8, half).wait_recv()


def local(planes, consts, pressure_source, solid_mask):
    anywhere = pl.BlockSpec(memory_space=pl.ANY)
    dma = pltpu.SemaphoreType.DMA
    source = pressure_source.reshape(64, 4, 8, 128).transpose(0, 2, 1, 3).reshape(64, 8, 4, 1, 128)
    mask = solid_mask.reshape(4, 8, 128).transpose(1, 0, 2).reshape(8, 4, 1, 128)
    out = pl.pallas_call(
        functools.partial(kernel, planes),
        out_shape=pltpu.VMEM(source.shape, F32),
        in_specs=[anywhere] * 5,
        out_specs=anywhere,
        scratch_shapes=[
            pltpu.VMEM((8, 64, 4, 1, 128), F32),
            pltpu.VMEM((NS, 512), BF16),
            pltpu.VMEM((NS, 512), BF16),
            pltpu.VMEM((2, MODES, NS), BF16),
            pltpu.VMEM((2, NS, MODES), BF16),
            pltpu.VMEM((2, MODES, 128), F32),
            pltpu.VMEM((4, MODES, 128), F32),
            pltpu.VMEM((MODES, 512), F32),
            pltpu.VMEM((4, MODES, 128), F32),
            pltpu.VMEM((2, MODES, 128), F32),
            pltpu.VMEM((6, 8, MODES), F32),
            pltpu.VMEM((6, 8, MODES), F32),
            pltpu.VMEM((MODES, 512), BF16),
            pltpu.VMEM((MODES, 512), BF16),
            pltpu.VMEM((8, 64, 4, 1, 128), F32),
            pltpu.VMEM((4, 1, 128), jnp.int32),
            dma((3, 8)), dma((3, 8)), dma((3, 8)), dma((3, 8)), dma((8,)), dma((8,)), dma((2,)), dma((10,)),
            pltpu.SemaphoreType.REGULAR,
        ],
        compiler_params=pltpu.CompilerParams(
            collective_id=0, has_side_effects=True, vmem_limit_bytes=40 * 1024 * 1024),
    )(*[pltpu.with_memory_space_constraint(v, pltpu.HBM) for v in (source, mask, *consts)])
    def copy_out(src, dst, sem):
        copies = [pltpu.make_async_copy(src.at[pl.ds(8 * i, 8)], dst.at[pl.ds(8 * i, 8)], sem.at[i]) for i in range(8)]
        for copy in copies:
            copy.start()
        for copy in copies:
            copy.wait()

    out = pl.pallas_call(
        copy_out, out_shape=pltpu.HBM(source.shape, F32), in_specs=[pl.BlockSpec(memory_space=pltpu.VMEM)], out_specs=anywhere,
        scratch_shapes=[dma((8,))])(pltpu.with_memory_space_constraint(out, pltpu.VMEM))
    return out.reshape(64, 8, 4, 128).transpose(0, 2, 1, 3).reshape(64, 4, 1024)


def solution(mesh):
    consts = tables()

    def step(pressure_source, solid_mask):
        return local(mesh.shape["plane"], [jnp.asarray(c) for c in consts], pressure_source, solid_mask)

    return jax.shard_map(
        step, mesh=mesh, in_specs=(P("span", "plane", None), P("plane", None)),
        out_specs=P("span", "plane", None), check_vma=False)
```
